32 devices in a mesh: seq: 2 (over x), col: 16 (over z, y, core).
Axes of the slice: x: 2, y: 2, z: 4, core: 2. Of those that a mesh axis runs over, the one named last changes fastest.
Arguments:
- alignment_embedding_tensor: bfloat16 [32, 128, 768], P('seq', 'col'), may hold values from -3 to 3
- horizontal_attention_triples: bfloat16 [32, 128, 2304], P('seq', 'col'), may hold values from -10 to 10
- occupancy_indicator: int32 [32, 128], P('seq', 'col'), may hold values from 0 to 1, as said below
- horizontal_attention_exit_matrix: bfloat16 [768, 768], P('col'), may hold values from -0.21875 to 0.21875
- vertical_attention_entry_matrix: bfloat16 [768, 2304], P('col'), may hold values from -0.43164062 to 0.43164062
- vertical_attention_exit_matrix: bfloat16 [768, 768], P('col'), may hold values from -0.21875 to 0.21875
- vertical_layernorm_scaling: float32 [768], replicated, may hold values from 0.25 to 1.75
Outputs:
- mixed: float32 [32, 128, 768], P('seq', 'col')
The draws below stay inside these ranges and needn't reach their ends.
Inputs may be any that keep to these rules, and one draw needn't show every extreme that they name: `occupancy_indicator`: every column holds a residue in some sequence.
All inputs are finite; a program needn't handle non-finite values.
Results may differ from the reference program's by a relative error of at most 0.035.
Values may be sent and summed in bfloat16 or wider, within the bound.
No kernel may reach another device: no remote copies, remote signals or barrier semaphores. Data moves between devices by JAX's collectives and lax.ppermute only.
A program may use at most 64 MiB of HBM per device.

```python
import math
import jax
import jax.numpy as jnp
from jax import lax

EMBED_DIMENSION = 768
H = 12
DH = 64
ALIGNED_PROTEINS = 32
ALIGNED_SITES = 128


def draw_horizontal_attention_triples(key, part):
    base = jnp.clip(jax.random.normal(key, (ALIGNED_PROTEINS, ALIGNED_SITES, 3 * EMBED_DIMENSION), jnp.float32), -5.5, 5.5)
    factor = jnp.concatenate((jnp.full((2 * EMBED_DIMENSION,), 1.7, jnp.float32), jnp.full((EMBED_DIMENSION,), 1.8, jnp.float32)))
    base = base * factor[None, None, :]
    base = jnp.clip(base, -10.0, 10.0)
    return base.astype(jnp.bfloat16)


def draw_occupancy_indicator(key, part):
    first, second, third, fourth, fifth = jax.random.split(jax.random.fold_in(key, 5), 5)
    start = jax.random.randint(first, (ALIGNED_PROTEINS, 1), ALIGNED_SITES // 3, ALIGNED_SITES // 2)
    length_unit = jax.random.randint(second, (ALIGNED_PROTEINS, 1), 0, ALIGNED_SITES // 16 + 1)
    boost = jnp.repeat(jax.random.randint(third, (ALIGNED_PROTEINS // 8, 1), 1, 5), 8, axis=0)
    length = length_unit * boost
    column = jnp.arange(ALIGNED_SITES, dtype=jnp.int32)[None, :]
    band = (column >= start) & (column < start + length)
    scattered = jax.random.randint(fourth, (ALIGNED_PROTEINS, ALIGNED_SITES), 0, 20) == 0
    keeper = jnp.repeat(jax.random.randint(fifth, (ALIGNED_PROTEINS // 8,), 0, 8), 8)
    keep_row = jnp.arange(ALIGNED_PROTEINS, dtype=jnp.int32) % 8 == keeper
    gap = (band | scattered) & jnp.logical_not(keep_row)[:, None]
    return jnp.where(gap, 0, 1).astype(jnp.int32)


def steps_of(own_key, extent, cuts, smallest, high):
    def one(dim, blocks):
        steps = jax.random.uniform(jax.random.fold_in(jax.random.fold_in(own_key, 6), dim), (blocks,), jnp.float32, smallest / len(cuts), high / len(cuts))
        return jnp.repeat(jnp.exp(steps), extent[dim] // blocks).reshape((-1,) + (1,) * (len(extent) - dim - 1))

    level = one(*cuts[0])
    for cut in cuts[1:]:
        level = level * one(*cut)
    return level


def normal_values(rng, extent, spread, limit, cuts=(), held_as=jnp.bfloat16):
    result = jax.random.normal(rng, extent, jnp.float32) * spread
    if len(cuts) > 0:
        result = steps_of(rng, extent, cuts, -0.22, 0.18) * result
    return jnp.clip(result, min=-limit, max=limit).astype(held_as)


def setup_inputs(seed: int = 0) -> dict:
    arg_keys = jax.random.split(jax.random.key(seed), 8)
    alignment_embedding_tensor = normal_values(arg_keys[0], (ALIGNED_PROTEINS, ALIGNED_SITES, EMBED_DIMENSION), 0.5, 3.0, ((0, 2), (1, 16)))
    horizontal_attention_triples = draw_horizontal_attention_triples(jax.random.fold_in(arg_keys[7], 71), 0)
    occupancy_indicator = draw_occupancy_indicator(jax.random.fold_in(arg_keys[7], 71), 0)
    horizontal_attention_exit_matrix = normal_values(arg_keys[3], (EMBED_DIMENSION, EMBED_DIMENSION), EMBED_DIMENSION ** -0.5, 0.21875, ((0, 16),))
    vertical_attention_entry_matrix = normal_values(arg_keys[4], (EMBED_DIMENSION, 3 * EMBED_DIMENSION), (2.0 / EMBED_DIMENSION ** 0.5), 0.43164062, ((0, 16),))
    vertical_attention_exit_matrix = normal_values(arg_keys[5], (EMBED_DIMENSION, EMBED_DIMENSION), EMBED_DIMENSION ** -0.5, 0.21875, ((0, 16),))
    vertical_layernorm_scaling = jnp.clip(1.0 + 0.15 * jax.random.normal(arg_keys[6], (EMBED_DIMENSION,), jnp.float32), 0.25, 1.75)
    return {"alignment_embedding_tensor": alignment_embedding_tensor, "horizontal_attention_triples": horizontal_attention_triples, "occupancy_indicator": occupancy_indicator, "horizontal_attention_exit_matrix": horizontal_attention_exit_matrix, "vertical_attention_entry_matrix": vertical_attention_entry_matrix, "vertical_attention_exit_matrix": vertical_attention_exit_matrix, "vertical_layernorm_scaling": vertical_layernorm_scaling}


def reference(alignment_embedding_tensor, horizontal_attention_triples, occupancy_indicator, horizontal_attention_exit_matrix, vertical_attention_entry_matrix, vertical_attention_exit_matrix, vertical_layernorm_scaling):
    live = occupancy_indicator.astype(jnp.float32)
    parts = horizontal_attention_triples.reshape(ALIGNED_PROTEINS, ALIGNED_SITES, 3, H, DH).astype(jnp.float32)
    query = parts[:, :, 0] * live[:, :, None, None]
    keys = parts[:, :, 1]
    values = parts[:, :, 2]
    scale = 1.0 / (math.sqrt(DH) * math.sqrt(ALIGNED_PROTEINS))
    logits = jnp.einsum('rihd,rjhd->hij', query, keys) * scale
    row_probs = jax.nn.softmax(logits, axis=-1).astype(jnp.bfloat16)
    row_context = jnp.einsum('hij,rjhd->rihd', row_probs.astype(jnp.float32), values).astype(jnp.bfloat16)
    merged_attended_heads = row_context.reshape(ALIGNED_PROTEINS * ALIGNED_SITES, EMBED_DIMENSION)
    skip_connection_hidden = alignment_embedding_tensor.reshape(ALIGNED_PROTEINS * ALIGNED_SITES, EMBED_DIMENSION).astype(jnp.float32) + jnp.dot(merged_attended_heads, horizontal_attention_exit_matrix, preferred_element_type=jnp.float32)
    center = skip_connection_hidden - lax.optimization_barrier(jnp.mean(skip_connection_hidden, axis=-1, keepdims=True))
    variance = lax.optimization_barrier(jnp.mean(center * center, axis=-1, keepdims=True))
    normed = (center * lax.rsqrt(variance + 1e-05) * vertical_layernorm_scaling).astype(jnp.bfloat16)
    col_qkv = jnp.dot(normed, vertical_attention_entry_matrix, preferred_element_type=jnp.float32).astype(jnp.bfloat16)
    col_qkv = col_qkv.reshape(ALIGNED_PROTEINS, ALIGNED_SITES, 3, H, DH)
    per_column = jnp.transpose(col_qkv, (1, 0, 2, 3, 4))
    live_columns = jnp.transpose(live, (1, 0))

    def attend(pieces):
        block, keep = pieces
        cq = block[:, 0].astype(jnp.float32)
        ck = block[:, 1].astype(jnp.float32)
        cv = block[:, 2].astype(jnp.float32)
        scores = jnp.einsum('rhd,shd->hrs', cq, ck) / math.sqrt(DH)
        scores = jnp.where(keep[None, None, :] > 0, scores, -1000000000.0)
        probs = jax.nn.softmax(scores, axis=-1).astype(jnp.bfloat16)
        return jnp.einsum('hrs,shd->rhd', probs.astype(jnp.float32), cv).astype(jnp.bfloat16)
    col_context = lax.map(attend, (per_column, live_columns))
    col_context = jnp.transpose(col_context, (1, 0, 2, 3)).reshape(ALIGNED_PROTEINS * ALIGNED_SITES, EMBED_DIMENSION)
    mixed = skip_connection_hidden + jnp.dot(col_context, vertical_attention_exit_matrix, preferred_element_type=jnp.float32)
    return mixed.reshape(ALIGNED_PROTEINS, ALIGNED_SITES, EMBED_DIMENSION)
```

```python
import functools
import math

import jax
import jax.numpy as jnp
from jax import lax
from jax.experimental import pallas as pl
from jax.experimental.pallas import tpu as pltpu
from jax.sharding import PartitionSpec as P

H = 12
DH = 64
F32 = jnp.float32
BF16 = jnp.bfloat16


def attend_columns(pieces):
    block, keep = pieces
    cq = block[..., :DH]
    ck = block[..., DH : 2 * DH]
    cv = block[..., 2 * DH :]
    scores = jnp.einsum("rgud,sgud->gurs", cq, ck, preferred_element_type=jnp.float32) / math.sqrt(
        DH
    )
    mask_keys = jnp.transpose(keep, (1, 2, 0))[:, :, None, :]
    scores = jnp.where(mask_keys > 0, scores, -1000000000.0)
    probs = jax.nn.softmax(scores, axis=-1).astype(jnp.bfloat16)
    return jnp.einsum("gurs,sgud->rgud", probs, cv, preferred_element_type=jnp.float32).astype(
        jnp.bfloat16
    )


def per_device_any(
    alignment_embedding_tensor,
    horizontal_attention_triples,
    occupancy_indicator,
    horizontal_attention_exit_matrix,
    vertical_attention_entry_matrix,
    vertical_attention_exit_matrix,
    vertical_layernorm_scaling,
):
    protein_extent, site_extent, embedding_dimension = alignment_embedding_tensor.shape
    total_rows = protein_extent * lax.axis_size("seq")
    live = occupancy_indicator.astype(jnp.bfloat16)
    parts = horizontal_attention_triples.reshape(protein_extent, site_extent, 3, H, DH)
    query = parts[:, :, 0] * live[:, :, None, None]
    keys = parts[:, :, 1]
    values = parts[:, :, 2]
    scale = 1.0 / (math.sqrt(DH) * math.sqrt(total_rows))
    full_wo_row, full_qkv, full_wo_col = (
        lax.all_gather(horizontal_attention_exit_matrix, "col", axis=0, tiled=True),
        lax.all_gather(vertical_attention_entry_matrix, "col", axis=0, tiled=True),
        lax.all_gather(vertical_attention_exit_matrix, "col", axis=0, tiled=True),
    )
    shard_portion = protein_extent * H // lax.axis_size("col")
    stacked = jnp.concatenate((query, keys, values), axis=-1)
    stacked = jnp.transpose(stacked, (1, 0, 2, 3)).reshape(site_extent, protein_extent * H, 3 * DH)
    moved = lax.all_to_all(stacked, "col", split_axis=1, concat_axis=0, tiled=True)
    unit_query = moved[..., :DH]
    unit_keys = moved[..., DH : 2 * DH]
    unit_values = moved[..., 2 * DH :]
    first_unit = lax.axis_index("col") * shard_portion
    head_of = (first_unit + jnp.arange(shard_portion, dtype=jnp.int32)) % H
    one_hot = (head_of[:, None] == jnp.arange(H, dtype=jnp.int32)[None, :]).astype(jnp.float32)
    unit_logits = jnp.einsum(
        "iud,jud->uij", unit_query, unit_keys, preferred_element_type=jnp.float32
    )
    partial_value = jnp.einsum("uh,uij->hij", one_hot, unit_logits) * scale
    logits = lax.psum(partial_value, ("seq", "col"))
    row_probs = jax.nn.softmax(logits, axis=-1).astype(jnp.bfloat16)
    unit_probs = jnp.einsum(
        "uh,hij->uij", one_hot.astype(jnp.bfloat16), row_probs, preferred_element_type=jnp.float32
    ).astype(jnp.bfloat16)
    unit_context = jnp.einsum(
        "uij,jud->iud", unit_probs, unit_values, preferred_element_type=jnp.float32
    ).astype(jnp.bfloat16)
    returned = lax.all_to_all(unit_context, "col", split_axis=0, concat_axis=1, tiled=True)
    context = jnp.transpose(returned.reshape(site_extent, protein_extent, H, DH), (1, 0, 2, 3))
    merged_attended_heads = context.reshape(protein_extent * site_extent, embedding_dimension)
    skip_connection_hidden = alignment_embedding_tensor.reshape(
        protein_extent * site_extent, embedding_dimension
    ).astype(jnp.float32) + jnp.dot(
        merged_attended_heads, full_wo_row, preferred_element_type=jnp.float32
    )
    center = skip_connection_hidden - jnp.mean(skip_connection_hidden, axis=-1, keepdims=True)
    variance = jnp.mean(center * center, axis=-1, keepdims=True)
    normed = (center * lax.rsqrt(variance + 1e-05) * vertical_layernorm_scaling).astype(
        jnp.bfloat16
    )
    col_qkv = jnp.dot(normed, full_qkv, preferred_element_type=jnp.float32).astype(jnp.bfloat16)
    seq_count = lax.axis_size("seq")
    units = site_extent * H // seq_count
    col_qkv = jnp.transpose(col_qkv.reshape(protein_extent, site_extent, 3, H, DH), (0, 1, 3, 2, 4))
    col_qkv = col_qkv.reshape(protein_extent, seq_count, units, 3 * DH)
    live_units = jnp.broadcast_to(live[:, :, None], (protein_extent, site_extent, H)).reshape(
        protein_extent, seq_count, units
    )
    attended = attend_columns(
        (
            lax.all_to_all(col_qkv, "seq", split_axis=1, concat_axis=0, tiled=True),
            lax.all_to_all(live_units, "seq", split_axis=1, concat_axis=0, tiled=True),
        )
    )
    returned_cols = lax.all_to_all(attended, "seq", split_axis=0, concat_axis=1, tiled=True)
    col_context = returned_cols.reshape(protein_extent * site_extent, embedding_dimension)
    mixed = skip_connection_hidden + jnp.dot(
        col_context, full_wo_col, preferred_element_type=jnp.float32
    )
    return mixed.reshape(protein_extent, site_extent, embedding_dimension)


VMEM = pl.BlockSpec(memory_space=pltpu.VMEM)
SMEM = pl.BlockSpec(memory_space=pltpu.SMEM)


def call(kernel, out, n_in, smem=0, scratch=(), in_specs=None, flops=0, moved=0, exps=0):
    return pl.pallas_call(
        kernel,
        out_shape=out,
        in_specs=in_specs or [SMEM] * smem + [VMEM] * (n_in - smem),
        out_specs=jax.tree.map(lambda _: VMEM, out),
        scratch_shapes=list(scratch),
        cost_estimate=pl.CostEstimate(flops=flops, bytes_accessed=moved, transcendentals=exps),
    )


def pack_kernel(groups, parts, x_ref, live_ref, o_ref):
    heads = H // groups
    per = x_ref.shape[0] // parts
    for t in range(3):
        for s in range(x_ref.shape[0]):
            part, r = divmod(s, per)
            row = x_ref[s, :, t * H * DH : (t + 1) * H * DH].astype(F32)
            if t == 0:
                row = row * live_ref[s]
            for g in range(groups):
                for h in range(heads):
                    piece = row[:, (g * heads + h) * DH : (g * heads + h + 1) * DH]
                    at = ((t * heads + h) * per + r) * DH
                    o_ref[g * parts + part, :, at : at + DH] = piece.astype(BF16)


def logits_kernel(heads, per, scale, side_ref, x_ref, keep_ref, send_ref):
    n = x_ref.shape[0]
    half = n // 2
    w = per * DH
    side = side_ref[0]
    for h in range(heads):
        k = x_ref[:, (heads + h) * w : (heads + h + 1) * w]
        for ref, part in ((keep_ref, side), (send_ref, 1 - side)):
            q = x_ref[pl.ds(pl.multiple_of(part * half, half), half), h * w : (h + 1) * w]
            ref[h] = (
                lax.dot_general(q, k, (((1,), (1,)), ((), ())), preferred_element_type=F32) * scale
            )


def add_kernel(a_ref, b_ref, o_ref):
    o_ref[...] = a_ref[...] + b_ref[...]


def softmax_kernel(a_ref, b_ref, c_ref, d_ref, o_ref):
    s = (a_ref[...] + b_ref[...]) + (c_ref[...] + d_ref[...])
    e = jnp.exp(s - jnp.max(s, axis=-1, keepdims=True))
    o_ref[...] = (e / jnp.sum(e, axis=-1, keepdims=True)).astype(BF16)


def context_kernel(heads, per, side_ref, x_ref, mine_ref, other_ref, o_ref):
    n = x_ref.shape[0]
    half = n // 2
    w = per * DH
    side = side_ref[0]
    for h in range(heads):
        v = x_ref[:, (2 * heads + h) * w : (2 * heads + h + 1) * w]
        for ref, part in ((mine_ref, side), (other_ref, 1 - side)):
            o = jnp.dot(ref[h], v, preferred_element_type=F32).astype(BF16)
            o_ref[pl.ds(pl.multiple_of(part * half, half), half), h * w : (h + 1) * w] = o


def residual_kernel(groups, parts, per, x_ref, emb_ref, w_ref, gain_ref, live_ref, res_ref, norm_ref, tmp_ref):
    heads = H // groups
    cols = x_ref.shape[1]
    tokens = parts * per * cols
    for g in range(groups):
        block = x_ref[g * parts : (g + 1) * parts].astype(F32)
        for h in range(heads):
            for r in range(per):
                at = (h * per + r) * DH
                to = (g * heads + h) * DH
                tmp_ref[:, r, :, to : to + DH] = block[:, :, at : at + DH]
    ctx = tmp_ref[...].reshape(tokens, H * DH).astype(BF16)
    res = emb_ref[...].astype(F32) + jnp.dot(ctx, w_ref[...], preferred_element_type=F32)
    res_ref[...] = res
    center = res - jnp.mean(res, axis=-1, keepdims=True)
    variance = jnp.mean(center * center, axis=-1, keepdims=True)
    norm = center * lax.rsqrt(variance + 1e-05) * gain_ref[...]
    norm_ref[:tokens] = norm.astype(BF16)
    norm_ref[tokens:] = jnp.broadcast_to(live_ref[...], (norm_ref.shape[0] - tokens, norm_ref.shape[1]))


def column_kernel(cols, a_ref, b_ref, wq_ref, wk_ref, wv_ref, mine_ref, send_ref):
    tokens = mine_ref.shape[0]
    x = jnp.concatenate((a_ref[:tokens], b_ref[:tokens]), axis=0)
    q, k, v = (
        jnp.dot(x, w[...], preferred_element_type=F32).astype(BF16) for w in (wq_ref, wk_ref, wv_ref)
    )
    n = 2 * tokens
    alive = jnp.concatenate(
        (a_ref[tokens : tokens + 1, :tokens], b_ref[tokens : tokens + 1, :tokens]), axis=1
    ).astype(F32)
    i = lax.broadcasted_iota(jnp.int32, (n, n), 0) % cols
    j = lax.broadcasted_iota(jnp.int32, (n, n), 1) % cols
    mask = (i == j) & (jnp.broadcast_to(alive, (n, n)) > 0)
    for h in range(q.shape[1] // DH):
        at = slice(h * DH, (h + 1) * DH)
        s = lax.dot_general(
            q[:, at], k[:, at], (((1,), (1,)), ((), ())), preferred_element_type=F32
        ) * (1.0 / math.sqrt(DH))
        s = jnp.where(mask, s, -1000000000.0)
        e = jnp.exp(s - jnp.max(s, axis=-1, keepdims=True))
        p = (e / jnp.sum(e, axis=-1, keepdims=True)).astype(BF16)
        o = jnp.dot(p, v[:, at], preferred_element_type=F32).astype(BF16)
        mine_ref[:, at] = o[:tokens]
        send_ref[:, at] = o[tokens:]


def project_kernel(side_ref, res_ref, ctx_ref, w_ref, o_ref):
    k = ctx_ref.shape[1]
    w = w_ref[pl.ds(pl.multiple_of(side_ref[0] * k, k), k), :]
    o_ref[...] = res_ref[...] + jnp.dot(ctx_ref[...], w, preferred_element_type=F32)


def per_device(groups, emb, triples, occupancy, wo_row, w_entry, wo_col, gain):
    seqs, cols, width = emb.shape
    n_seq, n_col = lax.axis_size("seq"), lax.axis_size("col")
    parts = n_col // groups
    heads, per = H // groups, seqs // parts
    sites, tokens = cols * n_col, seqs * cols
    scale = 1.0 / (math.sqrt(DH) * math.sqrt(seqs * n_seq))
    me_seq = lax.axis_index("seq")
    core = (lax.axis_index("col") % 2).astype(jnp.int32).reshape(1)
    side = me_seq.astype(jnp.int32).reshape(1)
    half = width // n_seq

    entry = w_entry.reshape(w_entry.shape[0], 3, width)
    entry = lax.dynamic_slice_in_dim(entry, me_seq * half, half, axis=2)
    packed_w = jnp.concatenate((wo_row, wo_col, entry.reshape(-1, 3 * half)), axis=1)
    full_w = lax.all_gather(packed_w, "col", axis=0, tiled=True)

    def swap_col(v, bit):
        return lax.ppermute(v, "col", [(i, i ^ bit) for i in range(n_col)])

    def swap_seq(v):
        return lax.ppermute(v, "seq", [(0, 1), (1, 0)])

    def swap_both(v, bit):
        n = n_seq * n_col
        return lax.ppermute(v, ("seq", "col"), [(i, (i + n_col) % n ^ bit) for i in range(n)])

    live = occupancy.astype(F32)
    live_rows = jnp.broadcast_to(live[:, :, None], (seqs, cols, H * DH))
    packed = call(
        functools.partial(pack_kernel, groups, parts),
        jax.ShapeDtypeStruct((n_col, cols, 3 * width // n_col * seqs), BF16),
        2,
        moved=4 * triples.size,
    )(triples, live_rows)
    moved = lax.all_to_all(packed, "col", split_axis=0, concat_axis=0, tiled=True)
    moved = moved.reshape(sites, 3 * heads * per * DH)

    part_shape = jax.ShapeDtypeStruct((heads, sites // 2, sites), F32)
    keep, send = call(
        functools.partial(logits_kernel, heads, per, scale),
        (part_shape, part_shape),
        2,
        smem=1,
        flops=2 * sites * sites * heads * per * DH,
    )(core, moved)
    part = call(add_kernel, part_shape, 2)(keep, swap_col(send, 1))
    probs = call(softmax_kernel, jax.ShapeDtypeStruct(part_shape.shape, BF16), 4)(
        part, swap_col(part, 2), swap_seq(part), swap_both(part, 2)
    )
    context = call(
        functools.partial(context_kernel, heads, per),
        jax.ShapeDtypeStruct((sites, heads * per * DH), BF16),
        4,
        smem=1,
    )(core, moved, probs, swap_col(probs, 1))
    returned = lax.all_to_all(
        context.reshape(n_col, cols, heads * per * DH), "col", split_axis=0, concat_axis=0, tiled=True
    )

    live_lanes = jnp.pad(live.reshape(1, tokens), ((0, 0), (0, width - tokens))).astype(BF16)
    w_block = lambda n, at: pl.BlockSpec((width, n), lambda i: (0, at))
    whole = lambda *shape: pl.BlockSpec(shape, lambda i: (0,) * len(shape))
    pad = 16
    res, norm = pl.pallas_call(
        functools.partial(residual_kernel, groups, parts, per),
        out_shape=(
            jax.ShapeDtypeStruct((tokens, width), F32),
            jax.ShapeDtypeStruct((tokens + pad, width), BF16),
        ),
        grid=(1,),
        in_specs=[
            whole(n_col, cols, heads * per * DH),
            whole(tokens, width),
            w_block(width, 0),
            whole(1, width),
            whole(1, width),
        ],
        out_specs=(whole(tokens, width), whole(tokens + pad, width)),
        scratch_shapes=[pltpu.VMEM((parts, per, cols, width), F32)],
    )(returned, emb.reshape(tokens, width), full_w, gain.reshape(1, width), live_lanes)

    ctx_shape = jax.ShapeDtypeStruct((tokens, half), BF16)
    mine, send = pl.pallas_call(
        functools.partial(column_kernel, cols),
        out_shape=(ctx_shape, ctx_shape),
        grid=(1,),
        in_specs=[
            whole(tokens + pad, width),
            whole(tokens + pad, width),
            w_block(half, 4),
            w_block(half, 5),
            w_block(half, 6),
        ],
        out_specs=(whole(tokens, half), whole(tokens, half)),
    )(norm, swap_seq(norm), full_w, full_w, full_w)

    def project(where, base, ctx):
        return pl.pallas_call(
            project_kernel,
            out_shape=jax.ShapeDtypeStruct((tokens, width), F32),
            grid=(1,),
            in_specs=[SMEM, whole(tokens, width), whole(tokens, half), w_block(width, 1)],
            out_specs=whole(tokens, width),
        )(where, base, ctx, full_w)

    other = swap_seq(send)
    out = project(1 - side, project(side, res, mine), other)
    return out.reshape(seqs, cols, width)


def solution(mesh):
    n_seq, n_col = mesh.shape["seq"], mesh.shape["col"]
    groups = 4
    body = per_device_any
    if n_seq == 2 and n_col % groups == 0 and n_col // groups >= 4:
        body = functools.partial(per_device, groups)
    placed = (
        P("seq", "col", None),
        P("seq", "col", None),
        P("seq", "col"),
        P("col", None),
        P("col", None),
        P("col", None),
        P(),
    )
    return jax.shard_map(
        body, mesh=mesh, in_specs=placed, out_specs=P("seq", "col", None), check_vma=False
    )
```
